32 devices in a mesh: dp: 8 (over z, x), tensor: 4 (over y, core).
Axes of the slice: x: 2, y: 2, z: 4, core: 2. Of those that a mesh axis runs over, the one named last changes fastest.
Arguments:
- tokens: bfloat16 [8192, 2048], P(('dp', 'tensor')), may hold values from -6 to 6
- cotangent: bfloat16 [8192, 2048], P(('dp', 'tensor')), may hold values from -6 to 6
- attn_gain: bfloat16 [2048], replicated, may hold values from 0.099609375 to 1.8984375
- q_gain: bfloat16 [128], replicated, may hold values from 0.099609375 to 1.8984375
- k_gain: bfloat16 [128], replicated, may hold values from 0.099609375 to 1.8984375
- w_query: bfloat16 [2048, 2048], P('dp', 'tensor'), may hold values from -0.125 to 0.125
- w_key: bfloat16 [2048, 1024], P('dp', 'tensor'), may hold values from -0.125 to 0.125
- w_value: bfloat16 [2048, 1024], P('dp', 'tensor'), may hold values from -0.125 to 0.125
- w_out: bfloat16 [2048, 2048], P('tensor', 'dp'), may hold values from -1 to 1
- mlp_gain: bfloat16 [2048], replicated, may hold values from 0.099609375 to 1.8984375
- w_gate: bfloat16 [2048, 6144], P('dp', 'tensor'), may hold values from -0.125 to 0.125
- w_up: bfloat16 [2048, 6144], P('dp', 'tensor'), may hold values from -0.125 to 0.125
- w_down: bfloat16 [6144, 2048], P('tensor', 'dp'), may hold values from -0.078125 to 0.078125
- segments: int32 [8192], P('dp'), may hold values from 0 to 3, as said below
- positions: int32 [8192], P('dp'), may hold values from 0 to 511, as said below
Outputs:
- output: bfloat16 [8192, 2048], P(('dp', 'tensor'))
- grad_tokens: bfloat16 [8192, 2048], P(('dp', 'tensor'))
- grad_w_query: float32 [2048, 2048], P('dp', 'tensor')
- grad_w_key: float32 [2048, 1024], P('dp', 'tensor')
- grad_w_value: float32 [2048, 1024], P('dp', 'tensor')
- grad_w_out: float32 [2048, 2048], P('tensor', 'dp')
- grad_w_gate: float32 [2048, 6144], P('dp', 'tensor')
- grad_w_up: float32 [2048, 6144], P('dp', 'tensor')
- grad_w_down: float32 [6144, 2048], P('tensor', 'dp')
- grad_attn_gain: float32 [2048], replicated
- grad_q_gain: float32 [128], replicated
- grad_k_gain: float32 [128], replicated
- grad_mlp_gain: float32 [2048], replicated
The draws below stay inside these ranges and needn't reach their ends.
Inputs may be any that keep to these rules, and one draw needn't show every extreme that they name: `segments`: within each sequence of 1024 tokens the numbers start at 0, never fall, and rise by one at each of the 3 document starts; every document has one token or more, and the last document of each sequence is its last 512 tokens. `positions`: the index of each token within its document.
All inputs are finite; a program needn't handle non-finite values.
Results may differ from the reference program's by a relative error of at most 0.014.
Values may be sent and summed in bfloat16 or wider, within the bound.
No kernel may reach another device: no remote copies, remote signals or barrier semaphores. Data moves between devices by JAX's collectives and lax.ppermute only.
A program may use at most 192 MiB of HBM per device.

```python
import math
import jax
import jax.numpy as jnp
from jax import lax

D = 2048
HQ = 16
HK = 8
HD = 128
FF = 6144
TOK_DP = 1024
DOCS = 4
TOKENS = 8192
N_DP = 8


def document_cuts(key):
    sequences = TOKENS // TOK_DP
    half = TOK_DP // 2
    base = jax.random.fold_in(key, 11)
    scores = jax.random.randint(base, (sequences, half - 1), 0, 2 ** 30 // TOK_DP) * TOK_DP
    scores = scores + jnp.arange(half - 1, dtype=jnp.int32)[None, :]
    picked = (lax.top_k(scores, DOCS - 2)[1] + 1).astype(jnp.int32)
    middle = jnp.full((sequences, 1), half, jnp.int32)
    return jnp.concatenate([picked, middle], 1).astype(jnp.int32)


def draw_segments(key, part):
    cuts = document_cuts(key)
    places = jnp.arange(TOK_DP, dtype=jnp.int32)
    numbers = jnp.sum((cuts[:, :, None] <= places[None, None, :]).astype(jnp.int32), 1)
    return numbers.reshape(TOKENS).astype(jnp.int32)


def draw_positions(key, part):
    cuts = document_cuts(key)
    places = jnp.arange(TOK_DP, dtype=jnp.int32)
    begins = jnp.max(jnp.where(cuts[:, :, None] <= places[None, None, :], cuts[:, :, None], 0), 1)
    return (places[None, :] - begins).reshape(TOKENS).astype(jnp.int32)


def with_spikes(drawn, own_key, source, target, shards_of, factor):
    owner, partner = [(jnp.arange(drawn.shape[axis_at]) // (drawn.shape[axis_at] // shards_of)).reshape([-1 if axis == axis_at else 1 for axis in range(drawn.ndim)]) for axis_at in (source, target)]
    chosen = jax.random.permutation(own_key, shards_of)[partner]
    strong = (owner == chosen) | (owner == (partner + shards_of // 2) % shards_of)
    return jnp.where(strong, factor * drawn, drawn)


def block_scale(key, dims, shards, least, high):
    level = 1.0
    for dim, shards_of in shards:
        steps = jax.random.uniform(jax.random.fold_in(jax.random.fold_in(key, 6), dim), (shards_of,), jnp.float32, least / len(shards), high / len(shards))
        level = level * jnp.repeat(jnp.exp(steps), dims[dim] // shards_of).reshape((-1,) + (1,) * (len(dims) - 1 - dim))
    return level


def normal_values(stream_key, extent, width, reach, split=(), held_as=jnp.bfloat16):
    drawn = width * jax.random.normal(stream_key, extent, jnp.float32)
    if split:
        drawn = drawn * block_scale(stream_key, extent, split, -0.22, 0.18)
    return jnp.clip(drawn, -reach, reach).astype(held_as)


def heavy_noise(key, dims, spread, most, pieces, heavy, kind=jnp.bfloat16):
    values = spread * jax.random.normal(key, dims, jnp.float32)
    if pieces:
        values = values * block_scale(key, dims, pieces, -0.22, 0.18)
    return jnp.clip(with_spikes(values, jax.random.fold_in(key, 3), *heavy), -most, most).astype(kind)


def setup_inputs(seed: int = 0) -> dict:
    seeds = jax.random.split(jax.random.key(seed), 16)
    return {
        "tokens": heavy_noise(seeds[0], (TOKENS, D), 1.0, 6.0, ((0, 32),), (0, 1, 32, 2.75)),
        "cotangent": heavy_noise(seeds[1], (TOKENS, D), 1.0, 6.0, ((0, 32),), (0, 1, 32, 2.75)),
        "attn_gain": jnp.clip(1.0 + 0.18 * jax.random.normal(seeds[2], (D,), jnp.float32), 0.099609375, 1.8984375).astype(jnp.bfloat16),
        "q_gain": jnp.clip(1.0 + 0.18 * jax.random.normal(seeds[3], (HD,), jnp.float32), 0.099609375, 1.8984375).astype(jnp.bfloat16),
        "k_gain": jnp.clip(1.0 + 0.18 * jax.random.normal(seeds[4], (HD,), jnp.float32), 0.099609375, 1.8984375).astype(jnp.bfloat16),
        "w_query": normal_values(seeds[5], (D, HQ * HD), D ** -0.5, 0.125, ((0, 8), (1, 4))),
        "w_key": normal_values(seeds[6], (D, HK * HD), D ** -0.5, 0.125, ((0, 8), (1, 4))),
        "w_value": normal_values(seeds[7], (D, HK * HD), D ** -0.5, 0.125, ((0, 8), (1, 4))),
        "w_out": normal_values(seeds[8], (HQ * HD, D), (HQ * HD // 64) ** -0.5, 1.0, ((0, 4), (1, 8))),
        "mlp_gain": jnp.clip(1.0 + 0.18 * jax.random.normal(seeds[9], (D,), jnp.float32), 0.099609375, 1.8984375).astype(jnp.bfloat16),
        "w_gate": normal_values(seeds[10], (D, FF), D ** -0.5, 0.125, ((0, 8), (1, 4))),
        "w_up": normal_values(seeds[11], (D, FF), D ** -0.5, 0.125, ((0, 8), (1, 4))),
        "w_down": normal_values(seeds[12], (FF, D), FF ** -0.5, 0.078125, ((0, 4), (1, 8))),
        "segments": draw_segments(jax.random.fold_in(seeds[15], 71), 0),
        "positions": draw_positions(jax.random.fold_in(seeds[15], 71), 0),
    }


EPS = 1e-06
THETA = 1000000.0

@jax.custom_vjp
def low(v):
    return lax.optimization_barrier(v.astype(jnp.bfloat16)).astype(jnp.float32)

@jax.custom_vjp
def low_back(v):
    return v

def low_keep(v):
    return (low(v), None)

def low_pass(kept, grad):
    return (grad,)

def back_keep(v):
    return (v, None)

def back_low(kept, grad):
    return (low(grad),)
low.defvjp(low_keep, low_pass)
low_back.defvjp(back_keep, back_low)

def norm_rows(values, gain):
    return values * lax.rsqrt(lax.optimization_barrier(jnp.mean(values * values, -1, keepdims=True)) + EPS) * gain

def rotary_tables(positions, head_size):
    half = head_size // 2
    freqs = jnp.exp(-math.log(THETA) * (2.0 * jnp.arange(half, dtype=jnp.float32)) / head_size)
    angles = positions.astype(jnp.float32)[:, None] * freqs[None, :]
    cosine = jnp.cos(angles)
    sine = jnp.sin(angles)
    return (jnp.concatenate([cosine, cosine], -1), jnp.concatenate([sine, sine], -1))

def rotate(values, cosine, sine):
    half = values.shape[-1] // 2
    turned = jnp.concatenate([-values[..., half:], values[..., :half]], -1)
    return values * cosine[:, None, :] + turned * sine[:, None, :]

def query_key_prep(query_raw, key_raw, query_gain, key_gain, cosine, sine, head_size):
    count = query_raw.shape[0]
    query = query_raw.reshape(count, -1, head_size)
    keys = key_raw.reshape(count, -1, head_size)
    return (rotate(norm_rows(query, query_gain), cosine, sine), rotate(norm_rows(keys, key_gain), cosine, sine))

def wide_dot(left, right):
    return jnp.dot(left, right, precision=lax.Precision.HIGHEST, preferred_element_type=jnp.float32)

def attend(query, keys, values, segments):
    length = query.shape[0]
    block = 512 if length % 512 == 0 else length
    starts = jnp.arange(length // block, dtype=jnp.int32) * block
    columns = jnp.arange(length, dtype=jnp.int32)
    grouped = query.reshape(length, HK, HQ // HK, HD)

    def one_block(start):
        query_blk = lax.dynamic_slice_in_dim(grouped, start, block, 0)
        seg_rows = lax.dynamic_slice_in_dim(segments, start, block, 0)
        row_index = start + jnp.arange(block, dtype=jnp.int32)
        allowed = (seg_rows[:, None] == segments[None, :]) & (row_index[:, None] >= columns[None, :])
        scores = jnp.einsum('qgrd,kgd->grqk', query_blk, keys, precision=lax.Precision.HIGHEST)
        scores = low_back(scores * (1.0 / math.sqrt(HD)))
        masked = jnp.where(allowed, scores, -jnp.inf)
        peak = lax.optimization_barrier(jnp.max(masked, -1, keepdims=True))
        expo = jnp.exp(masked - peak)
        probs = expo / lax.optimization_barrier(jnp.sum(expo, -1, keepdims=True))
        return jnp.einsum('grqk,kgd->qgrd', low(probs), values, precision=lax.Precision.HIGHEST)
    attended = lax.map(jax.checkpoint(one_block), starts)
    return attended.reshape(length, HQ * HD)

def layer(resid_in, params, segments, positions):
    gain_one, query_gain, key_gain, query_w, key_w, value_w, out_w, gain_two, gate_w, up_w, down_w = params
    count = resid_in.shape[0]
    sequences = count // TOK_DP
    normed_one = low(norm_rows(resid_in, gain_one))
    query_raw = low_back(wide_dot(normed_one, query_w))
    key_raw = low_back(wide_dot(normed_one, key_w))
    value_rows = low(low_back(wide_dot(normed_one, value_w)))
    cosine, sine = rotary_tables(positions, HD)
    query, keys = query_key_prep(query_raw, key_raw, query_gain, key_gain, cosine, sine, HD)
    query = low(query)
    keys = low(keys)
    attended = jax.vmap(attend)(query.reshape(sequences, TOK_DP, HQ, HD), keys.reshape(sequences, TOK_DP, HK, HD), value_rows.reshape(sequences, TOK_DP, HK, HD), segments.reshape(sequences, TOK_DP))
    attended = low(low_back(attended.reshape(count, HQ * HD)))
    resid_mid = resid_in + low_back(wide_dot(attended, out_w))
    normed_two = low(norm_rows(resid_mid, gain_two))
    gate = low_back(wide_dot(normed_two, gate_w))
    up = low_back(wide_dot(normed_two, up_w))
    hidden = low(jax.nn.silu(gate) * up)
    return resid_mid + low_back(wide_dot(hidden, down_w))

def reference(tokens, cotangent, attn_gain, q_gain, k_gain, w_query, w_key, w_value, w_out, mlp_gain, w_gate, w_up, w_down, segments, positions):
    params = tuple((item.astype(jnp.float32) for item in (attn_gain, q_gain, k_gain, w_query, w_key, w_value, w_out, mlp_gain, w_gate, w_up, w_down)))
    group = math.gcd(N_DP, max(1, 4096 // TOK_DP))
    turns = N_DP // group
    inputs = tokens.astype(jnp.float32).reshape(turns, group * TOK_DP, D)
    grads_out = cotangent.astype(jnp.float32).reshape(turns, group * TOK_DP, D)
    seg_all = segments.reshape(turns, group * TOK_DP)
    pos_all = positions.reshape(turns, group * TOK_DP)

    def one_turn(totals, item):
        resid_in, grad_out, seg_part, pos_part = item

        def run(values, weights):
            return layer(values, weights, seg_part, pos_part)
        result, pull = jax.vjp(run, resid_in, params)
        grad_in, grad_params = pull(grad_out)
        totals = tuple((first + second for first, second in zip(totals, grad_params)))
        return (totals, (result, grad_in))
    zeros = tuple((jnp.zeros_like(item) for item in params))
    totals, (results, grads_in) = lax.scan(one_turn, zeros, (inputs, grads_out, seg_all, pos_all))
    output = results.reshape(TOKENS, D).astype(jnp.bfloat16)
    grad_tokens = grads_in.reshape(TOKENS, D).astype(jnp.bfloat16)
    return (output, grad_tokens, totals[3], totals[4], totals[5], totals[6], totals[8], totals[9], totals[10], totals[0], totals[1], totals[2], totals[7])
```

```python
import math

import jax
import jax.numpy as jnp
from jax import lax
from jax.sharding import PartitionSpec as P

EPS = 1e-06
THETA = 1000000.0
F32 = jnp.float32
BF16 = jnp.bfloat16
DEPTH = 2


def norm_rows(values, gain):
    return values * lax.rsqrt(jnp.mean(values * values, -1, keepdims=True) + EPS) * gain


def rotary_tables(positions, head_size):
    half = head_size // 2
    freqs = jnp.exp(-math.log(THETA) * (2.0 * jnp.arange(half, dtype=F32)) / head_size)
    angles = positions.astype(F32)[:, None] * freqs[None, :]
    cosine = jnp.cos(angles)
    sine = jnp.sin(angles)
    return (jnp.concatenate([cosine, cosine], -1), jnp.concatenate([sine, sine], -1))


def rotate(values, cosine, sine):
    half = values.shape[-1] // 2
    turned = jnp.concatenate([-values[..., half:], values[..., :half]], -1)
    return values * cosine[:, None, :] + turned * sine[:, None, :]


def query_key_prep(query_raw, key_raw, query_gain, key_gain, cosine, sine, head_size):
    count = query_raw.shape[0]
    query = query_raw.reshape(count, -1, head_size)
    keys = key_raw.reshape(count, -1, head_size)
    return (
        rotate(norm_rows(query, query_gain), cosine, sine),
        rotate(norm_rows(keys, key_gain), cosine, sine),
    )


class Ring:
    def __init__(self, size):
        self.size = size
        self.order = list(range(0, size, 2)) + list(range(size - 1, 0, -2))
        self.ahead = [(self.order[i], self.order[(i + 1) % size]) for i in range(size)]
        self.back = [(b, a) for a, b in self.ahead]
        self.mid = size // 2
        self.rel = [0]
        for s in range(1, self.mid):
            self.rel += [-s, s]
        self.rel.append(self.mid)

    def blocks(self):
        n = self.size
        me = lax.axis_index("dp")
        place = jnp.where(me % 2 == 0, me // 2, n - 1 - me // 2)
        spot = (place + jnp.array(self.rel, jnp.int32) + n) % n
        index = jnp.where(spot < n // 2, 2 * spot, 2 * (n - 1 - spot) + 1)
        wanted = jnp.arange(n, dtype=jnp.int32)
        spots = jnp.where(wanted % 2 == 0, wanted // 2, n - 1 - wanted // 2)
        away = (spots - place + n) % n
        inverse = jnp.where(
            away == 0,
            0,
            jnp.where(
                away == self.mid,
                n - 1,
                jnp.where(away < self.mid, 2 * away, 2 * (n - away) - 1),
            ),
        )
        return index, inverse


def pick_blocks(values, index, axis):
    count = index.shape[0]
    width = values.shape[axis] // count
    return jnp.concatenate(
        [
            lax.dynamic_slice_in_dim(values, index[k] * width, width, axis)
            for k in range(count)
        ],
        axis,
    )


class Queue:
    def __init__(self):
        self.past = []

    def enter(self, arrays):
        if len(self.past) >= DEPTH:
            held = self.past[-DEPTH]
            arrays, held = lax.optimization_barrier((arrays, held))
        return arrays

    def leave(self, arrays):
        self.past.append(arrays)


def gather_steps(ring, queue, shard):
    ahead = back = shard
    found = [shard]
    for _ in range(1, ring.mid):
        ahead, back = queue.enter((ahead, back))
        ahead = lax.ppermute(ahead, "dp", ring.ahead)
        back = lax.ppermute(back, "dp", ring.back)
        queue.leave((ahead, back))
        found += [ahead, back]
        yield
    half = shard.shape[0] // 2
    ahead, back = queue.enter((ahead[:half], back[half:]))
    ahead = lax.ppermute(ahead, "dp", ring.ahead)
    back = lax.ppermute(back, "dp", ring.back)
    queue.leave((ahead, back))
    found.append(jnp.concatenate([ahead, back], 0))
    yield
    return found


def scatter_steps(ring, queue, chunks):
    mid = ring.mid
    far = chunks[-1]
    half = far.shape[0] // 2
    ahead, back = far[:half], far[half:]
    for s in range(mid, 0, -1):
        ahead, back = queue.enter((ahead, back))
        ahead = lax.ppermute(ahead, "dp", ring.ahead)
        back = lax.ppermute(back, "dp", ring.back)
        queue.leave((ahead, back))
        yield
        if s > 1:
            to_ahead, to_back = chunks[2 * (s - 1)], chunks[2 * (s - 1) - 1]
            if s == mid:
                ahead = jnp.concatenate([to_ahead[:half] + ahead, to_ahead[half:]], 0)
                back = jnp.concatenate([to_back[:half], to_back[half:] + back], 0)
            else:
                ahead, back = to_ahead + ahead, to_back + back
    own = chunks[0].astype(F32)
    if mid == 1:
        total = own + jnp.concatenate([ahead, back], 0).astype(F32)
    else:
        total = own + ahead.astype(F32) + back.astype(F32)
    return total


def advance(step):
    try:
        next(step)
    except StopIteration as end:
        return end.value
    return None


def run_all(steps):
    results = [None] * len(steps)
    live = []
    waiting = list(range(len(steps)))
    while waiting or live:
        while waiting and len(live) < DEPTH:
            live.append(waiting.pop(0))
        for i in list(live):
            value = advance(steps[i])
            if value is not None:
                results[i] = value
                live.remove(i)
    return results


def partner(bit, size):
    return [(i, i ^ bit) for i in range(size)]


def spread_rows(values, size):
    blocks = {0: values}
    bit = size // 2
    while bit:
        for r, block in list(blocks.items()):
            blocks[r ^ bit] = lax.ppermute(block, "tensor", partner(bit, size))
        bit //= 2
    return jnp.concatenate([blocks[r] for r in range(size)], 0)


def sum_rows(values, size):
    rows = values.shape[0] // size
    blocks = {r: values[r * rows : (r + 1) * rows] for r in range(size)}
    bit = 1
    while bit < size:
        for r in [r for r in blocks if not r & bit]:
            other = lax.ppermute(blocks.pop(r | bit), "tensor", partner(bit, size))
            total = blocks[r].astype(F32) + other.astype(F32)
            blocks[r] = total if bit * 2 == size else total.astype(BF16)
        bit *= 2
    return blocks[0]


def all_sum(values, mesh_shape):
    for axis in ("tensor", "dp"):
        bit = 1
        while bit < mesh_shape[axis]:
            values = values + lax.ppermute(values, axis, partner(bit, mesh_shape[axis]))
            bit *= 2
    return values


def make_on_device(mesh_shape):
    n_dp, n_tensor = mesh_shape["dp"], mesh_shape["tensor"]
    ring = Ring(n_dp)

    def on_device(
        tokens,
        cotangent,
        attn_gain,
        q_gain,
        k_gain,
        w_query,
        w_key,
        w_value,
        w_out,
        mlp_gain,
        w_gate,
        w_up,
        w_down,
        segments,
        positions,
    ):
        head_size = q_gain.shape[0]
        length = segments.shape[0]
        rows = length // n_tensor
        scale = 1.0 / math.sqrt(head_size)
        index, inverse = ring.blocks()
        q_width, k_width = w_query.shape[1], w_key.shape[1]

        queue = Queue()
        qkv_shard = jnp.concatenate([w_query, w_key, w_value], 1)
        qkv_parts, out_parts, gate_parts, up_parts, down_parts = run_all(
            [gather_steps(ring, queue, w) for w in (qkv_shard, w_out, w_gate, w_up, w_down)]
        )

        resid_in = pick_blocks(tokens, index, 1).astype(F32)
        cot_own = pick_blocks(cotangent, index, 1)
        gain_one = pick_blocks(attn_gain, index, 0).astype(F32)
        gain_two = pick_blocks(mlp_gain, index, 0).astype(F32)
        query_scale = q_gain.astype(F32)
        key_scale = k_gain.astype(F32)

        mine = lax.axis_index("tensor")
        places = jnp.concatenate(
            [(mine ^ r) * rows + jnp.arange(rows, dtype=jnp.int32) for r in range(n_tensor)]
        )
        seg_rel = jnp.concatenate(
            [lax.dynamic_slice_in_dim(segments, (mine ^ r) * rows, rows, 0) for r in range(n_tensor)]
        )
        pos_rel = jnp.concatenate(
            [lax.dynamic_slice_in_dim(positions, (mine ^ r) * rows, rows, 0) for r in range(n_tensor)]
        )

        normed_one = norm_rows(resid_in, gain_one).astype(BF16)
        gathered_one = spread_rows(normed_one, n_tensor)
        grad_rows = spread_rows(cot_own, n_tensor)

        qkv_w = jnp.concatenate(qkv_parts, 0)
        qkv = jnp.dot(gathered_one, qkv_w, preferred_element_type=F32)
        query_raw = qkv[:, :q_width]
        key_raw = qkv[:, q_width : q_width + k_width]
        value_rows = qkv[:, q_width + k_width :].astype(BF16)
        cosine, sine = rotary_tables(pos_rel, head_size)

        def prep(query_in, key_in, query_gain, key_gain):
            return query_key_prep(query_in, key_in, query_gain, key_gain, cosine, sine, head_size)

        (query_rot, key_rot), pull_prep = jax.vjp(prep, query_raw, key_raw, query_scale, key_scale)
        kv_heads = key_rot.shape[1]

        span = length // 2
        query_b = query_rot.astype(BF16).reshape(2, span, kv_heads, -1, head_size)
        keys_b = key_rot.astype(BF16).reshape(2, span, kv_heads, head_size)
        values_b = value_rows.reshape(2, span, kv_heads, head_size)
        seg_half = seg_rel.reshape(2, span)
        place_half = places.reshape(2, span)
        allowed = (seg_half[:, :, None] == seg_half[:, None, :]) & (
            place_half[:, :, None] >= place_half[:, None, :]
        )
        allowed = allowed[:, None, None]
        scores = (
            jnp.einsum("bqgrd,bkgd->bgrqk", query_b, keys_b, preferred_element_type=F32) * scale
        )
        masked = jnp.where(allowed, scores, -jnp.inf)
        peak = jnp.max(masked, -1, keepdims=True)
        expo = jnp.exp(masked - peak)
        total = jnp.sum(expo, -1, keepdims=True)
        probs = expo / total
        probs_b = probs.astype(BF16)
        attended = jnp.einsum("bgrqk,bkgd->bqgrd", probs_b, values_b, preferred_element_type=F32)
        attended_b = attended.reshape(length, -1).astype(BF16)

        out_w = jnp.concatenate(out_parts, 1)
        resid_mid = resid_in + sum_rows(
            jnp.dot(attended_b, out_w, preferred_element_type=F32).astype(BF16), n_tensor
        )
        normed_two = norm_rows(resid_mid, gain_two).astype(BF16)
        gathered_two = spread_rows(normed_two, n_tensor)
        gate_w = jnp.concatenate(gate_parts, 0)
        up_w = jnp.concatenate(up_parts, 0)
        down_w = jnp.concatenate(down_parts, 1)
        gate = jnp.dot(gathered_two, gate_w, preferred_element_type=F32)
        up = jnp.dot(gathered_two, up_w, preferred_element_type=F32)
        sigma = jax.nn.sigmoid(gate)
        swish = gate * sigma
        hidden = (swish * up).astype(BF16)

        grad_down = jnp.einsum("sf,sd->fd", hidden, grad_rows, preferred_element_type=F32).astype(BF16)
        grad_hidden = jnp.einsum("sd,fd->sf", grad_rows, down_w, preferred_element_type=F32)
        grad_gate = (grad_hidden * up * sigma * (1.0 + gate * (1.0 - sigma))).astype(BF16)
        grad_up = (grad_hidden * swish).astype(BF16)
        grad_normed_two = sum_rows(
            (
                jnp.einsum("sf,df->sd", grad_gate, gate_w, preferred_element_type=F32)
                + jnp.einsum("sf,df->sd", grad_up, up_w, preferred_element_type=F32)
            ).astype(BF16),
            n_tensor,
        )
        grad_gate_w = jnp.einsum(
            "sd,sf->df", gathered_two, grad_gate, preferred_element_type=F32
        ).astype(BF16)
        grad_up_w = jnp.einsum(
            "sd,sf->df", gathered_two, grad_up, preferred_element_type=F32
        ).astype(BF16)
        result = resid_mid + sum_rows(
            jnp.dot(hidden, down_w, preferred_element_type=F32).astype(BF16), n_tensor
        )
        _, pull_two = jax.vjp(norm_rows, resid_mid, gain_two)
        back_mid, grad_gain_two = pull_two(grad_normed_two)
        grad_mid = cot_own.astype(F32) + back_mid
        grad_rows_one = spread_rows(grad_mid.astype(BF16), n_tensor)
        grad_out_w = jnp.einsum(
            "sq,sd->qd", attended_b, grad_rows_one, preferred_element_type=F32
        ).astype(BF16)
        grad_attended = (
            jnp.einsum("sd,qd->sq", grad_rows_one, out_w, preferred_element_type=F32)
            .astype(BF16)
            .reshape(2, span, kv_heads, -1, head_size)
        )
        grad_values = jnp.einsum(
            "bgrqk,bqgrd->bkgd", probs_b, grad_attended, preferred_element_type=F32
        )
        grad_probs = jnp.einsum(
            "bqgrd,bkgd->bgrqk", grad_attended, values_b, preferred_element_type=F32
        )
        inner = jnp.sum(probs * grad_probs, -1, keepdims=True)
        grad_scores = (probs * (grad_probs - inner)).astype(BF16)
        grad_queries = (
            jnp.einsum("bgrqk,bkgd->bqgrd", grad_scores, keys_b, preferred_element_type=F32) * scale
        )
        grad_keys = (
            jnp.einsum("bgrqk,bqgrd->bkgd", grad_scores, query_b, preferred_element_type=F32) * scale
        )
        grad_query_raw, grad_key_raw, grad_q_scale, grad_k_scale = pull_prep(
            (
                grad_queries.reshape(length, -1, head_size),
                grad_keys.reshape(length, -1, head_size),
            )
        )
        grad_qkv = jnp.concatenate(
            [
                grad_query_raw.astype(BF16),
                grad_key_raw.astype(BF16),
                grad_values.reshape(length, -1).astype(BF16),
            ],
            1,
        )
        grad_qkv_w = jnp.einsum(
            "sd,sq->dq", gathered_one, grad_qkv, preferred_element_type=F32
        ).astype(BF16)
        grad_normed_one = sum_rows(
            jnp.einsum("sq,dq->sd", grad_qkv, qkv_w, preferred_element_type=F32).astype(BF16),
            n_tensor,
        )

        def by_rows(grad):
            size = grad.shape[0] // n_dp
            return [grad[k * size : (k + 1) * size] for k in range(n_dp)]

        def by_columns(grad):
            size = grad.shape[1] // n_dp
            return [grad[:, k * size : (k + 1) * size] for k in range(n_dp)]

        queue = Queue()
        sum_down, sum_gate, sum_up, sum_out, sum_qkv = run_all(
            [
                scatter_steps(ring, queue, chunks)
                for chunks in (
                    by_columns(grad_down),
                    by_rows(grad_gate_w),
                    by_rows(grad_up_w),
                    by_columns(grad_out_w),
                    by_rows(grad_qkv_w),
                )
            ]
        )

        _, pull_one = jax.vjp(norm_rows, resid_in, gain_one)
        back_in, grad_gain_one = pull_one(grad_normed_one)
        grad_tokens = (grad_mid + back_in).astype(BF16)
        width = resid_in.shape[1]
        gains = jnp.concatenate(
            [
                pick_blocks(grad_gain_one, inverse, 0),
                pick_blocks(grad_gain_two, inverse, 0),
                grad_q_scale,
                grad_k_scale,
            ]
        )
        gains = all_sum(gains.reshape(-1, head_size), mesh_shape).reshape(-1)
        return (
            pick_blocks(result.astype(BF16), inverse, 1),
            pick_blocks(grad_tokens, inverse, 1),
            sum_qkv[:, :q_width],
            sum_qkv[:, q_width : q_width + k_width],
            sum_qkv[:, q_width + k_width :],
            sum_out,
            sum_gate,
            sum_up,
            sum_down,
            gains[:width],
            gains[2 * width : 2 * width + head_size],
            gains[2 * width + head_size :],
            gains[width : 2 * width],
        )

    return on_device


def solution(mesh):
    placed = (
        P(("dp", "tensor"), None),
        P(("dp", "tensor"), None),
        P(),
        P(),
        P(),
        P("dp", "tensor"),
        P("dp", "tensor"),
        P("dp", "tensor"),
        P("tensor", "dp"),
        P(),
        P("dp", "tensor"),
        P("dp", "tensor"),
        P("tensor", "dp"),
        P("dp"),
        P("dp"),
    )
    return jax.shard_map(
        make_on_device(dict(mesh.shape)),
        mesh=mesh,
        in_specs=placed,
        out_specs=(
            P(("dp", "tensor"), None),
            P(("dp", "tensor"), None),
            P("dp", "tensor"),
            P("dp", "tensor"),
            P("dp", "tensor"),
            P("tensor", "dp"),
            P("dp", "tensor"),
            P("dp", "tensor"),
            P("tensor", "dp"),
            P(),
            P(),
            P(),
            P(),
        ),
        check_vma=False,
    )
```
